32 devices in a mesh: wide: 16 (over z, x, core), narrow: 2 (over y).
Axes of the slice: x: 2, y: 2, z: 4, core: 2. Of those that a mesh axis runs over, the one named last changes fastest.
Arguments:
- inputs: bfloat16 [32, 512, 768], P(('wide', 'narrow')), may hold values from -6 to 6
- segment_ids: int32 [32, 512], P(('wide', 'narrow')), may hold values from 0 to 128, as said below
- qkv_weight: bfloat16 [3, 768, 768], P(None, ('wide', 'narrow')), may hold values from -0.21875 to 0.21875
- out_weight: bfloat16 [768, 768], P(('wide', 'narrow')), may hold values from -0.875 to 0.875
- up_weight: bfloat16 [768, 3072], P(('wide', 'narrow')), may hold values from -0.21875 to 0.21875
- down_weight: bfloat16 [3072, 768], P(('wide', 'narrow')), may hold values from -0.109375 to 0.109375
- biases: bfloat16 [6, 768], P(None, ('wide', 'narrow')), may hold values from -3 to 3
- gains: bfloat16 [2, 768], P(None, ('wide', 'narrow')), may hold values from 0.5 to 1.5
- up_bias: bfloat16 [3072], P(('wide', 'narrow')), may hold values from -3 to 3
- out_grad: bfloat16 [32, 512, 768], P(('wide', 'narrow')), may hold values from -6 to 6
Outputs:
- activations: bfloat16 [32, 512, 768], P(('wide', 'narrow'))
- grad_input: float32 [32, 512, 768], P(('wide', 'narrow'))
- grad_qkv: float32 [3, 768, 768], P(None, ('wide', 'narrow'))
- grad_out_weight: float32 [768, 768], P(('wide', 'narrow'))
- grad_up_weight: float32 [768, 3072], P(('wide', 'narrow'))
- grad_down_weight: float32 [3072, 768], P(('wide', 'narrow'))
- grad_biases: float32 [6, 768], P(None, ('wide', 'narrow'))
- grad_gains: float32 [2, 768], P(None, ('wide', 'narrow'))
- grad_up_bias: float32 [3072], P(('wide', 'narrow'))
The draws below stay inside these ranges and needn't reach their ends.
Inputs may be any that keep to these rules, and one draw needn't show every extreme that they name: `segment_ids`: in each row, ids rise by 0 or 1 from token to token starting at 1, never above 128, and a nonempty run of padding tokens with id 0 ends the row; some row reaches 128.
All inputs are finite; a program needn't handle non-finite values.
Results may differ from the reference program's by a relative error of at most 0.012.
The reference program's roundings to bfloat16 on the way count: a program that leaves them out, or rounds other values in their place, can miss the bound.
Values may be sent and summed in bfloat16 or wider, within the bound.
A program may use at most 192 MiB of HBM per device.

```python
import jax
import jax.numpy as jnp
from jax import lax

D = 768
HEADS = 12
HEAD_DIM = 64
FF = 3072
SEQ = 512
ROWS = 32


def draw_segment_ids(key, part):
    key_starts, key_pads, key_pick = jax.random.split(jax.random.fold_in(key, 7), 3)
    position = jnp.arange(SEQ, dtype=jnp.int32)[None, :]
    row_index = jnp.arange(ROWS, dtype=jnp.int32)[:, None]
    chosen = jax.random.randint(key_pick, (), 0, ROWS)
    special = row_index == chosen
    random_starts = jax.random.randint(key_starts, (ROWS, SEQ), 0, 96) == 0
    every_fourth = position % 4 == 0
    starts = jnp.where(special, every_fourth, random_starts) & (position > 0)
    doc_ids = jnp.minimum(1 + jnp.cumsum(starts.astype(jnp.int32), axis=1), SEQ // 4)
    pad_len = jax.random.randint(key_pads, (ROWS, 1), 1, SEQ // 4 + 1)
    pad_len = jnp.where(special, 1, pad_len)
    return jnp.where(position >= SEQ - pad_len, 0, doc_ids).astype(jnp.int32)


def spiked(array, key, source, target, parts, factor):
    def block_of(dim):
        return (jnp.arange(array.shape[dim]) // (array.shape[dim] // parts)).reshape((-1,) + (1,) * (array.ndim - 1 - dim))

    near = jax.random.permutation(key, parts)[block_of(target)]
    second = (block_of(target) + parts // 2) % parts
    return jnp.where((block_of(source) == near) | (block_of(source) == second), factor * array, array)


def shard_levels(stream_key, shape, cuts, smallest, largest):
    def one(dim, parts):
        draws = jax.random.uniform(jax.random.fold_in(jax.random.fold_in(stream_key, 6), dim), (parts,), jnp.float32, smallest / len(cuts), largest / len(cuts))
        return jnp.repeat(jnp.exp(draws), shape[dim] // parts).reshape((-1,) + (1,) * (len(shape) - dim - 1))

    level = one(*cuts[0])
    for cut in cuts[1:]:
        level = level * one(*cut)
    return level


def normal_values(key, dims, scale, limit, shards=(), kind=jnp.bfloat16):
    result = scale * jax.random.normal(key, dims, jnp.float32)
    if shards:
        result = result * shard_levels(key, dims, shards, -0.22, 0.18)
    return jnp.clip(result, -limit, limit).astype(kind)


def heavy_noise(rng, extent, deviation, limit, cuts, heavy, kind=jnp.bfloat16):
    result = deviation * jax.random.normal(rng, extent, jnp.float32)
    if cuts:
        result = result * shard_levels(rng, extent, cuts, -0.22, 0.18)
    return jnp.clip(spiked(result, jax.random.fold_in(rng, 3), *heavy), -limit, limit).astype(kind)


def setup_inputs(seed: int = 0) -> dict:
    keys = jax.random.split(jax.random.key(seed), 11)
    inputs = heavy_noise(keys[0], (ROWS, SEQ, D), 1.0, 6.0, ((0, 32),), (0, 2, 32, 2.75))
    segment_ids = draw_segment_ids(jax.random.fold_in(keys[10], 71), 0)
    qkv_weight = normal_values(keys[2], (3, D, D), D ** -0.5, 0.21875, ((1, 32),))
    out_weight = normal_values(keys[3], (D, D), (D // 16) ** -0.5, 0.875, ((0, 32),))
    up_weight = normal_values(keys[4], (D, FF), D ** -0.5, 0.21875, ((0, 32),))
    down_weight = normal_values(keys[5], (FF, D), FF ** -0.5, 0.109375, ((0, 32),))
    biases = normal_values(keys[6], (6, D), 0.5, 3.0, ((1, 32),))
    gains = jnp.clip(1.0 + 0.1 * jax.random.normal(keys[7], (2, D), jnp.float32), 0.5, 1.5).astype(jnp.bfloat16)
    up_bias = normal_values(keys[8], (FF,), 0.5, 3.0, ((0, 32),))
    out_grad = normal_values(keys[9], (ROWS, SEQ, D), 1.0, 6.0, ((0, 32),))
    return {"inputs": inputs, "segment_ids": segment_ids, "qkv_weight": qkv_weight, "out_weight": out_weight, "up_weight": up_weight, "down_weight": down_weight, "biases": biases, "gains": gains, "up_bias": up_bias, "out_grad": out_grad}


@jax.custom_vjp
def low(v):
    return lax.optimization_barrier(v.astype(jnp.bfloat16)).astype(jnp.float32)

@jax.custom_vjp
def low_back(v):
    return v

def low_keep(v):
    return (low(v), None)

def low_pass(kept, grad):
    return (grad,)

def back_keep(v):
    return (v, None)

def back_low(kept, grad):
    return (low(grad),)
low.defvjp(low_keep, low_pass)
low_back.defvjp(back_keep, back_low)
norm_eps = 1e-12

def matmul(left, right):
    return jnp.dot(left, right, preferred_element_type=jnp.float32, precision=lax.Precision.HIGHEST)

def layer_norm(values, gain_vec, shift_vec):
    centre = values - lax.optimization_barrier(jnp.mean(values, axis=-1, keepdims=True))
    variance = lax.optimization_barrier(jnp.mean(centre * centre, axis=-1, keepdims=True))
    return centre * lax.rsqrt(variance + norm_eps) * gain_vec + shift_vec

def one_row(params, row_in, row_ids):
    qkv_w, out_w, up_w, down_w, bias_all, gain_all, up_shift = params
    queries = low(low_back(matmul(row_in, qkv_w[0]) + bias_all[0]))
    key_rows = low(low_back(matmul(row_in, qkv_w[1])))
    value_rows = low(low_back(matmul(row_in, qkv_w[2]) + bias_all[1]))
    head_shape = (SEQ, HEADS, HEAD_DIM)
    scores = jnp.einsum('qhd,khd->hqk', queries.reshape(head_shape), key_rows.reshape(head_shape), precision=lax.Precision.HIGHEST) * HEAD_DIM ** (-0.5)
    same_doc = row_ids[:, None] == row_ids[None, :]
    scores = low_back(jnp.where(same_doc[None], scores, -1e+30))
    attn_probs = low(jax.nn.softmax(scores, axis=-1))
    mixed_out = jnp.einsum('hqk,khd->qhd', attn_probs, value_rows.reshape(head_shape), precision=lax.Precision.HIGHEST).reshape(SEQ, D)
    mixed_out = low(low_back(mixed_out))
    branch = low_back(matmul(mixed_out, out_w) + bias_all[2])
    normed_one = layer_norm(row_in + branch, gain_all[0], bias_all[3])
    hidden_pre = low_back(matmul(low(normed_one), up_w) + up_shift)
    act_low = low(jax.nn.gelu(hidden_pre, approximate=False))
    feed_out = low_back(matmul(act_low, down_w) + bias_all[4])
    return layer_norm(normed_one + feed_out, gain_all[1], bias_all[5])

def forward(params, inputs, segment_ids):

    def row_step(state_val, row_pair):
        return (state_val, one_row(params, row_pair[0], row_pair[1]))
    _, output = lax.scan(jax.checkpoint(row_step), jnp.zeros((), jnp.float32), (inputs, segment_ids))
    return output

def reference(inputs, segment_ids, qkv_weight, out_weight, up_weight, down_weight, biases, gains, up_bias, out_grad):
    params = tuple((item.astype(jnp.float32) for item in (qkv_weight, out_weight, up_weight, down_weight, biases, gains, up_bias)))
    inputs_f = inputs.astype(jnp.float32)

    def whole(inputs_in, qkv_w, out_w, up_w, down_w, bias_all, gain_all, up_shift):
        return forward((qkv_w, out_w, up_w, down_w, bias_all, gain_all, up_shift), inputs_in, segment_ids)
    output, pullback = jax.vjp(whole, inputs_f, *params)
    all_grads = pullback(out_grad.astype(jnp.float32))
    return (output.astype(jnp.bfloat16), all_grads[0], all_grads[1], all_grads[2], all_grads[3], all_grads[4], all_grads[5], all_grads[6], all_grads[7])
```

```python
import functools
import types

import jax
import jax.numpy as jnp
from jax import lax
from jax.experimental import pallas as pl
from jax.experimental.pallas import tpu as pltpu
from jax.sharding import PartitionSpec as P

MESH = pl.DeviceIdType.MESH
f32 = jnp.float32
bf = jnp.bfloat16
HEADS = 12
HEAD_DIM = 64


norm_eps = 1e-12
score_scale = 0.125


def layer_norm(values, gain_vec, shift_vec):
    centre = values - jnp.mean(values, axis=-1, keepdims=True)
    variance = jnp.mean(centre * centre, axis=-1, keepdims=True)
    rstd_val = lax.rsqrt(variance + norm_eps)
    norm_hat = centre * rstd_val
    return (norm_hat * gain_vec + shift_vec, norm_hat, rstd_val)


def norm_back(grad_in, norm_hat, rstd_val, gain_vec):
    scaled = grad_in * gain_vec
    return rstd_val * (
        scaled
        - jnp.mean(scaled, axis=-1, keepdims=True)
        - norm_hat * jnp.mean(scaled * norm_hat, axis=-1, keepdims=True)
    )


def gelu_slope(hidden_pre):
    cumul = 0.5 * (1.0 + lax.erf(hidden_pre * 0.7071067811865476))
    return cumul + hidden_pre * jnp.exp(-0.5 * hidden_pre * hidden_pre) * 0.3989422804014327


def head_scores(query_row, key_row, id_row):
    scores = (
        jnp.einsum("qhd,khd->hqk", query_row, key_row, preferred_element_type=jnp.float32)
        * score_scale
    )
    same_doc = id_row[:, None] == id_row[None, :]
    return jnp.where(same_doc[None], scores, -1e30)


def attend_row(pieces):
    query_row, key_row, value_row, id_row = pieces
    scores = head_scores(query_row, key_row, id_row)
    row_peak = jnp.max(scores, axis=-1, keepdims=True)
    exp_terms = jnp.exp(scores - row_peak)
    row_total = jnp.sum(exp_terms, axis=-1, keepdims=True)
    probs_low = (exp_terms / row_total).astype(jnp.bfloat16)
    mixed_row = jnp.einsum(
        "hqk,khd->qhd", probs_low, value_row, preferred_element_type=jnp.float32
    ).astype(jnp.bfloat16)
    return (mixed_row, row_peak + jnp.log(row_total))


def attend_back(pieces):
    query_row, key_row, value_row, id_row, log_total, grad_row = pieces
    scores = head_scores(query_row, key_row, id_row)
    attn_probs = jnp.exp(scores - log_total)
    probs_low = attn_probs.astype(jnp.bfloat16)
    prob_grad = jnp.einsum("qhd,khd->hqk", grad_row, value_row, preferred_element_type=jnp.float32)
    value_grad = jnp.einsum("hqk,qhd->khd", probs_low, grad_row, preferred_element_type=jnp.float32)
    inner = jnp.sum(prob_grad * attn_probs, axis=-1, keepdims=True)
    score_grad = (attn_probs * (prob_grad - inner)).astype(jnp.bfloat16)
    query_grad = (
        jnp.einsum("hqk,khd->qhd", score_grad, key_row, preferred_element_type=jnp.float32)
        * score_scale
    )
    key_grad = (
        jnp.einsum("hqk,qhd->khd", score_grad, query_row, preferred_element_type=jnp.float32)
        * score_scale
    )
    return (
        query_grad.astype(jnp.bfloat16),
        key_grad.astype(jnp.bfloat16),
        value_grad.astype(jnp.bfloat16),
    )


def run_forward(inputs, segment_ids, params):
    qkv_w, out_w, up_w, down_w, bias_all, gain_all, up_shift = params
    row_count, seq_len, model_width = inputs.shape
    flat_in = inputs.reshape(row_count * seq_len, model_width)
    bias_f = bias_all.astype(jnp.float32)
    gain_f = gain_all.astype(jnp.float32)
    projected = jnp.einsum("nd,cde->cne", flat_in, qkv_w, preferred_element_type=jnp.float32)
    queries = (projected[0] + bias_f[0]).astype(jnp.bfloat16)
    key_rows = projected[1].astype(jnp.bfloat16)
    value_rows = (projected[2] + bias_f[1]).astype(jnp.bfloat16)
    head_shape = (row_count, seq_len, HEADS, HEAD_DIM)
    heads_in = (
        queries.reshape(head_shape),
        key_rows.reshape(head_shape),
        value_rows.reshape(head_shape),
        segment_ids,
    )
    mixed_rows, log_total = lax.map(attend_row, heads_in)
    mixed_low = mixed_rows.reshape(row_count * seq_len, model_width)
    branch = jnp.dot(mixed_low, out_w, preferred_element_type=jnp.float32) + bias_f[2]
    normed_one, hat_one, rstd_one = layer_norm(
        flat_in.astype(jnp.float32) + branch, gain_f[0], bias_f[3]
    )
    first_low = normed_one.astype(jnp.bfloat16)
    hidden_pre = jnp.dot(first_low, up_w, preferred_element_type=jnp.float32) + up_shift.astype(
        jnp.float32
    )
    act_low = jax.nn.gelu(hidden_pre, approximate=False).astype(jnp.bfloat16)
    feed_out = jnp.dot(act_low, down_w, preferred_element_type=jnp.float32) + bias_f[4]
    output, hat_two, rstd_two = layer_norm(normed_one + feed_out, gain_f[1], bias_f[5])
    return (
        output,
        heads_in,
        log_total,
        mixed_low,
        hat_one,
        rstd_one,
        first_low,
        hidden_pre,
        act_low,
        hat_two,
        rstd_two,
    )


def layer(inputs, segment_ids, gathered, out_grad):
    row_count, seq_len, model_width = inputs.shape
    qkv_w, out_w, up_w, down_w, bias_all, gain_all, up_shift = gathered
    gain_f = gain_all.astype(jnp.float32)
    (
        output,
        heads_in,
        log_total,
        mixed_low,
        hat_one,
        rstd_one,
        first_low,
        hidden_pre,
        act_low,
        hat_two,
        rstd_two,
    ) = run_forward(inputs, segment_ids, gathered)
    activations = output.astype(jnp.bfloat16).reshape(row_count, seq_len, model_width)
    flat_in = inputs.reshape(row_count * seq_len, model_width)
    top_grad = out_grad.reshape(row_count * seq_len, model_width).astype(jnp.float32)
    gain_two_grad = jnp.sum(top_grad * hat_two, axis=0)
    shift_two_grad = jnp.sum(top_grad, axis=0)
    grad_h2 = norm_back(top_grad, hat_two, rstd_two, gain_f[1])
    feed_grad = grad_h2.astype(jnp.bfloat16)
    grad_down = jnp.einsum("nf,nd->fd", act_low, feed_grad, preferred_element_type=jnp.float32)
    down_bias_grad = jnp.sum(feed_grad.astype(jnp.float32), axis=0)
    act_grad = jnp.einsum("nd,fd->nf", feed_grad, down_w, preferred_element_type=jnp.float32)
    hidden_grad = (act_grad * gelu_slope(hidden_pre)).astype(jnp.bfloat16)
    grad_up = jnp.einsum("nd,nf->df", first_low, hidden_grad, preferred_element_type=jnp.float32)
    up_bias_grad = jnp.sum(hidden_grad.astype(jnp.float32), axis=0)
    grad_first = grad_h2 + jnp.einsum(
        "nf,df->nd", hidden_grad, up_w, preferred_element_type=jnp.float32
    )
    gain_one_grad = jnp.sum(grad_first * hat_one, axis=0)
    shift_one_grad = jnp.sum(grad_first, axis=0)
    grad_h1 = norm_back(grad_first, hat_one, rstd_one, gain_f[0])
    branch_grad = grad_h1.astype(jnp.bfloat16)
    grad_out = jnp.einsum("nd,ne->de", mixed_low, branch_grad, preferred_element_type=jnp.float32)
    out_bias_grad = jnp.sum(branch_grad.astype(jnp.float32), axis=0)
    mixed_grad = jnp.einsum(
        "ne,de->nd", branch_grad, out_w, preferred_element_type=jnp.float32
    ).astype(jnp.bfloat16)
    head_shape = (row_count, seq_len, HEADS, HEAD_DIM)
    query_rows, key_rows, value_rows, id_rows = heads_in
    query_grad, key_grad, value_grad = lax.map(
        attend_back,
        (query_rows, key_rows, value_rows, id_rows, log_total, mixed_grad.reshape(head_shape)),
    )
    flat_shape = (row_count * seq_len, model_width)
    qkv_grad = jnp.stack(
        [
            query_grad.reshape(flat_shape),
            key_grad.reshape(flat_shape),
            value_grad.reshape(flat_shape),
        ]
    )
    grad_qkv = jnp.einsum("nd,cne->cde", flat_in, qkv_grad, preferred_element_type=jnp.float32)
    qkv_bias_grad = jnp.sum(qkv_grad.astype(jnp.float32), axis=1)
    grad_in = grad_h1 + jnp.einsum(
        "cne,cde->nd", qkv_grad, qkv_w, preferred_element_type=jnp.float32
    )
    grad_bias_rows = jnp.stack(
        [
            qkv_bias_grad[0],
            qkv_bias_grad[2],
            out_bias_grad,
            shift_one_grad,
            down_bias_grad,
            shift_two_grad,
        ]
    )
    grad_gain_rows = jnp.stack([gain_one_grad, gain_two_grad])
    grad_input = grad_in.reshape(row_count, seq_len, model_width)
    return (
        activations,
        grad_input,
        (grad_qkv, grad_out, grad_up, grad_down, grad_bias_rows, grad_gain_rows, up_bias_grad),
    )


AXES = ("wide", "narrow")


def body_any(inputs, segment_ids, qkv_weight, out_weight, up_weight, down_weight, biases, gains, up_bias, out_grad):
    dims = (1, 0, 0, 0, 1, 1, 0)
    params = (qkv_weight, out_weight, up_weight, down_weight, biases, gains, up_bias)
    gathered = tuple(lax.all_gather(a, AXES, axis=d, tiled=True) for a, d in zip(params, dims))
    activations, grad_input, grads = layer(inputs, segment_ids, gathered, out_grad)
    shares = tuple(lax.psum_scatter(g, AXES, scatter_dimension=d, tiled=True) for g, d in zip(grads, dims))
    return (activations, grad_input, *shares)


EPS=1e-12
def nn(a,b): return lax.dot_general(a,b,(((1,),(0,)),((),())),preferred_element_type=f32)
def nt(a,b): return lax.dot_general(a,b,(((1,),(1,)),((),())),preferred_element_type=f32)
def tn(a,b): return lax.dot_general(a,b,(((0,),(0,)),((),())),preferred_element_type=f32)
def cols(n,w): return pl.ds(pl.multiple_of(n*w,128),w)
def rows(n,w): return pl.ds(pl.multiple_of(n*w,8),w)
def gelu_both(u):
    cdf=0.5*(1.0+lax.erf(u*0.7071067811865476))
    return u*cdf, cdf+u*jnp.exp(-0.5*u*u)*0.3989422804014327

class Layer:
    def __init__(self,r,loop):
        self.r=types.SimpleNamespace(**r)
        self.loop=loop
    def prepare(self):
        row=self.r.seg[0:1,:].astype(f32)
        self.r.segc[...]=jnp.broadcast_to(row,(128,512)).T
    def qkv(self):
        def body(t):
            c=t//3; n=t%3
            a=nn(self.r.x[...],self.r.w4[c,:,cols(n,256)])
            b=jnp.where(c==0,self.r.brow[0:1,cols(n,256)],jnp.where(c==2,self.r.brow[1:2,cols(n,256)],0.0))
            self.r.q3[c,:,cols(n,256)]=((a+b)*jnp.where(c==0,0.125,1.0)).astype(bf)
        self.loop(9,body,"qkv")
    def transpose(self,src,dst,name):
        def body(n): dst[rows(n,128),:]=src[:,cols(n,128)].T
        self.loop(6,body,name)
    def attend(self):
        def body(hp):
            L=cols(hp,128)
            kp=self.r.q3[1,:,L]
            vt=self.r.q3[2,:,L].T
            lane=lax.broadcasted_iota(jnp.int32,(512,128),1)
            for h in range(2):
                kz=jnp.where((lane>=64)==(h==1),kp,jnp.zeros_like(kp))
                for c in range(2):
                    Q=slice(c*256,c*256+256)
                    s=nt(kz,self.r.q3[0,Q,L])
                    same=jnp.concatenate([self.r.segc[...]]*2,axis=1)==self.r.seg[0:1,Q].astype(f32)
                    s=jnp.where(same,s,-1e30)
                    m=jnp.max(s,axis=0,keepdims=True)
                    e=jnp.exp(s-m)
                    l=jnp.sum(e,axis=0,keepdims=True)
                    p=(e*(1.0/l)).astype(bf)
                    self.r.pt[hp*2+h,:,Q]=p
                    o=nn(vt[h*64:h*64+64,:],p)
                    self.r.mt[pl.ds(pl.multiple_of(hp*128+h*64,64),64),Q]=o.astype(bf)
            self.r.a1[:,L]=self.r.mt[rows(hp,128),:].T
        self.loop(6,body,"attend")
    def out_proj(self):
        def body(n):
            C=cols(n,256)
            self.r.h[:,C]=nn(self.r.a1[...],self.r.w4[3,:,C])+self.r.brow[2:3,C]+self.r.x[:,C].astype(f32)
        self.loop(3,body,"out")
    def norm_one(self):
        g=self.r.brow[6:7,:]; s=self.r.brow[3:4,:]; b=self.r.brow[4:5,:]
        def body(i):
            R=rows(i,64)
            v=self.r.h[R,:]
            c=v-jnp.mean(v,axis=-1,keepdims=True)
            r=lax.rsqrt(jnp.mean(c*c,axis=-1,keepdims=True)+EPS)
            hat=c*r
            self.r.hat[R,:]=hat
            self.r.r1[R,:]=jnp.broadcast_to(r,(64,128))
            first=hat*g+s
            self.r.a0[R,:]=first.astype(bf)
            self.r.h[R,:]=first+b
        self.loop(8,body,"norm1")
    def up_proj(self):
        def body(t):
            n=t//3; C=cols(t%3,256)
            u=nn(self.r.a0[...],self.r.up[n,:,C])+self.r.upb[n,0:1,C]
            a,g=gelu_both(u)
            a=a.astype(bf)
            self.r.act[n,:,C]=a
            self.r.g[n,rows(t%3,256),0:512]=a.T
            self.r.gp[n,:,C]=g.astype(self.r.gp.dtype)
        self.loop(12,body,"up")
    def down_proj(self,panel=lambda m:m):
        def body(m):
            n=panel(m)
            for k in range(3):
                C=slice(k*256,k*256+256)
                self.r.h[:,C]+=nn(self.r.act[n],self.r.dn[n,:,C])
        self.loop(4,body,"down")
    def norm_two(self):
        g=self.r.brow[7:8,:]; s=self.r.brow[5:6,:]
        self.r.sums[...]=jnp.zeros_like(self.r.sums)
        def body(i):
            R=rows(i,64)
            v=self.r.h[R,:]
            c=v-jnp.mean(v,axis=-1,keepdims=True)
            r=lax.rsqrt(jnp.mean(c*c,axis=-1,keepdims=True)+EPS)
            hat=c*r
            self.r.o_act[R,:]=(hat*g+s).astype(bf)
            e=self.r.dy[R,:].astype(f32)
            eg=e*g
            d=r*(eg-jnp.mean(eg,axis=-1,keepdims=True)-hat*jnp.mean(eg*hat,axis=-1,keepdims=True))
            self.r.h[R,:]=d
            low=d.astype(bf)
            self.r.a1[R,:]=low
            self.r.sums[4:5,:]+=jnp.sum(low.astype(f32),axis=0,keepdims=True)
            self.r.sums[5:6,:]+=jnp.sum(e,axis=0,keepdims=True)
            self.r.sums[7:8,:]+=jnp.sum(e*hat,axis=0,keepdims=True)
        self.loop(8,body,"norm2")
    def down_grad(self,panel=lambda m:m):
        def body(t):
            R=rows(t%3,256); n=panel(t//3)
            self.r.g[n,R,:]=nn(self.r.g[n,R,0:512],self.r.a1[...]).astype(bf)
        self.loop(12,body,"gdn")
    def down_back(self):
        def body(t):
            n=t//3; C=cols(t%3,256)
            d=nt(self.r.a1[...],self.r.dn[n,rows(t%3,256),:])
            low=(d*self.r.gp[n,:,C].astype(f32)).astype(bf)
            self.r.act[n,:,C]=low
            self.r.gub[n,0:1,C]=jnp.sum(low.astype(f32),axis=0,keepdims=True)
        self.loop(12,body,"dact")
    def up_back(self):
        def body(n):
            C=cols(n,256)
            acc=nt(self.r.act[0],self.r.up[0,rows(n,256),:])
            for p in range(1,4): acc=acc+nt(self.r.act[p],self.r.up[p,rows(n,256),:])
            self.r.h[:,C]+=acc
        self.loop(3,body,"uback")
    def up_grad(self):
        def body(t):
            n=t//3; C=cols(t%3,256)
            self.r.dn[n,:,C]=nn(self.r.ft[...],self.r.act[n,:,C]).astype(bf)
        self.loop(12,body,"ugrad")
    def norm_one_back(self):
        g=self.r.brow[6:7,:]
        def body(i):
            R=rows(i,64)
            e=self.r.h[R,:]; hat=self.r.hat[R,:]; r=self.r.r1[R,0:1]
            eg=e*g
            d=r*(eg-jnp.mean(eg,axis=-1,keepdims=True)-hat*jnp.mean(eg*hat,axis=-1,keepdims=True))
            self.r.h[R,:]=d
            low=d.astype(bf)
            self.r.a0[R,:]=low
            self.r.sums[2:3,:]+=jnp.sum(low.astype(f32),axis=0,keepdims=True)
            self.r.sums[3:4,:]+=jnp.sum(e,axis=0,keepdims=True)
            self.r.sums[6:7,:]+=jnp.sum(e*hat,axis=0,keepdims=True)
        self.loop(8,body,"n1b")
    def out_back(self):
        def body(n):
            C=cols(n,256)
            self.r.a1[:,C]=nt(self.r.a0[...],self.r.w4[3,rows(n,256),:]).astype(bf)
            self.r.up[3,:,C]=nn(self.r.mt[...],self.r.a0[:,C]).astype(bf)
        self.loop(3,body,"oback")
    def attend_back(self,start,n,name):
        def body(i):
            hp=start+i
            L=cols(hp,128)
            kp=self.r.q3[1,:,L]; vp=self.r.q3[2,:,L]
            kt=kp.T
            lane=lax.broadcasted_iota(jnp.int32,(512,128),1)
            dv=[];dk=[]
            for h in range(2):
                vz=jnp.where((lane>=64)==(h==1),vp,jnp.zeros_like(vp))
                av=ak=None
                for c in range(2):
                    Q=slice(c*256,c*256+256)
                    dm=self.r.a1[Q,L]
                    d=nt(vz,dm)
                    pb=self.r.pt[hp*2+h,:,Q]
                    p=pb.astype(f32)
                    inner=jnp.sum(d*p,axis=0,keepdims=True)
                    ds=(p*(d-inner)).astype(bf)
                    v=nn(pb,dm); k=nn(ds,self.r.q3[0,Q,L])
                    av=v if av is None else av+v
                    ak=k if ak is None else ak+k
                    self.r.dqt[h*64:h*64+64,Q]=nn(kt[h*64:h*64+64,:],ds)*0.125
                dv.append(av);dk.append(ak)
            first=lane<64
            dvv=jnp.where(first,dv[0],dv[1]).astype(bf); dkk=jnp.where(first,dk[0],dk[1]).astype(bf)
            dqq=self.r.dqt[...].T.astype(bf)
            self.r.q3[0,:,L]=dqq; self.r.q3[1,:,L]=dkk; self.r.q3[2,:,L]=dvv
            self.r.sums[0:1,L]=jnp.sum(dqq.astype(f32),axis=0,keepdims=True)
            self.r.sums[1:2,L]=jnp.sum(dvv.astype(f32),axis=0,keepdims=True)
        self.loop(n,body,name)
    def qkv_grad(self,start,n,name):
        def body(t):
            c=t//n; C=cols(start+t%n,256)
            self.r.up[c,:,C]=nn(self.r.xt[...],self.r.q3[c,:,C]).astype(bf)
        self.loop(3*n,body,name)
    def input_grad(self):
        def body(n):
            C=cols(n,256); R=rows(n,256)
            acc=nt(self.r.q3[0],self.r.w4[0,R,:])
            for c in range(1,3): acc=acc+nt(self.r.q3[c],self.r.w4[c,R,:])
            self.r.h[:,C]+=acc
        self.loop(3,body,"igrad")

def layer_scratch():
    V=pltpu.VMEM
    return dict(segc=V((512,128),f32),q3=V((3,512,768),bf),pt=V((12,512,512),bf),mt=V((768,512),bf),xt=V((768,512),bf),ft=V((768,512),bf),
      a0=V((512,768),bf),a1=V((512,768),bf),hat=V((512,768),f32),r1=V((512,128),f32),act=V((4,512,768),bf),gp=V((4,512,768),bf),dqt=V((128,512),f32))


def coords():
    w = lax.axis_index("wide")
    return w // 4, (w // 2) % 2, w % 2, lax.axis_index("narrow")


def dev(z, x, c, y):
    return ((z * 2 + x) * 2 + c, y)


def block_of(z, x, c, y):
    return ((z * 2 + x) * 2 + c) * 2 + y


def neighbours():
    z, x, c, y = coords()
    return dict(x=dev(z, 1 - x, c, y), y=dev(z, x, c, 1 - y), c=dev(z, x, 1 - c, y), u=dev(z + 1, x, c, y), d=dev(z - 1, x, c, y))


def entry_barrier(z, x, c, y):
    bar = pltpu.get_barrier_semaphore()
    for d in (dev(z, 1 - x, c, y), dev(z, x, c, 1 - y), dev(z, x, 1 - c, y)):
        pl.semaphore_signal(bar, inc=1, device_id=d, device_id_type=MESH)

    @pl.when(z < 3)
    def _():
        pl.semaphore_signal(bar, inc=1, device_id=dev(z + 1, x, c, y), device_id_type=MESH)

    @pl.when(z > 0)
    def _():
        pl.semaphore_signal(bar, inc=1, device_id=dev(z - 1, x, c, y), device_id_type=MESH)

    pl.semaphore_wait(bar, 3 + jnp.where(z < 3, 1, 0) + jnp.where(z > 0, 1, 0))


def near(z, j):
    m = jnp.minimum(z, 3 - z)
    b = m if j == 0 else 1 - m if j == 1 else j
    return jnp.where(z < 2, b, 3 - b)


def block_ref(ref, p, b, half=None, n=1):
    if p == 3:
        return ref.at[pl.ds(b, n)] if n > 1 else ref.at[b]
    C = pl.ds(0, 768) if half is None else pl.ds(half * 384, 384)
    if p == 2:
        return ref.at[b // 8, pl.ds(pl.multiple_of((b % 8) * 96, 8), 96 * n), C]
    return ref.at[:, pl.ds(pl.multiple_of(b * 24, 8), 24 * n), C]


def with_small(p):
    return (p, 3) if p == 0 else (p,)


def remote(src, dst, ssem, rsem, to):
    return pltpu.make_async_remote_copy(
        src_ref=src, dst_ref=dst, send_sem=ssem, recv_sem=rsem, device_id=to, device_id_type=MESH
    )


class Pending:
    def start(self, make, when=None):
        if when is None:
            make().start()
        else:
            pl.when(when())(lambda: make().start())
        self.sends.append((when, make))

    def drain(self):
        for when, make in self.sends:
            if when is None:
                make().wait_send()
            else:
                pl.when(when())(lambda make=make: make().wait_send())
        self.sends = []


class Gather(Pending):
    def __init__(self, arrays, ssem, rsem, csem):
        self.sends = []
        self.a, self.ssem, self.rsem, self.csem = arrays, ssem, rsem, csem
        self.z, self.x, self.c, self.y = coords()
        self.to = neighbours()

    def copy(self, p, j, xr, yr, slot, core=False, half=None, to="c", sslot=0, from_core=None):
        z, x, c, y = self.z, self.x, self.c, self.y
        zz = near(z, j)
        b = block_of(zz, 1 - x if xr else x, c if from_core is None else from_core, 1 - y if yr else y)
        r = block_ref(self.a[p], p, b, half)
        sem = self.csem if core else self.rsem
        return remote(r, r, self.ssem.at[p, j, sslot], sem.at[p, zz, slot], self.to[to])

    def send(self, *a, when=None, **k):
        self.start(lambda: self.copy(*a, **k), when)

    def S(self, p, j):
        z = self.z
        for q in with_small(p):
            if j > 0:
                self.copy(q, j, 0, 0, 0, to="x", sslot=2).wait_recv()
            self.send(q, j, 0, 0, 1, to="x", sslot=2)
            self.send(q, j, 0, 0, 2, to="y", sslot=3)
            self.send(q, j, 0, 0, 0, to="u", sslot=0, when=lambda: jnp.logical_and(z < 3, near(z, j) <= z))
            self.send(q, j, 0, 0, 0, to="d", sslot=1, when=lambda: jnp.logical_and(z > 0, near(z, j) >= z))
            self.send(q, j, 0, 0, 0, core=True, sslot=4)

    def T(self, p, j):
        for q in with_small(p):
            self.copy(q, j, 1, 0, 1, to="x", sslot=2).wait_recv()
            self.send(q, j, 1, 0, 3, half=0 if q < 3 else None, to="y", sslot=6)
            self.copy(q, j, 0, 1, 2, to="y", sslot=3).wait_recv()
            if q < 3:
                self.send(q, j, 0, 1, 4, half=1, to="x", sslot=5)
            self.send(q, j, 1, 0, 1, core=True, sslot=7)
            self.send(q, j, 0, 1, 2, core=True, sslot=8)

    def U(self, p, j):
        for q in with_small(p):
            self.copy(q, j, 1, 1, 3, half=0 if q < 3 else None, to="y", sslot=6).wait_recv()
            if q < 3:
                self.copy(q, j, 1, 1, 4, half=1, to="x", sslot=5).wait_recv()
            self.send(q, j, 1, 1, 3, core=True, sslot=9)

    def W(self, p, j):
        for q in with_small(p):
            for k, (xr, yr) in enumerate(((0, 0), (1, 0), (0, 1), (1, 1))):
                self.copy(q, j, xr, yr, k, core=True, sslot=4, from_core=1 - self.c).wait_recv()


RC, RDA, RDB, RX, RY, RU, RD = 0, 2, 3, 4, 5, 6, 7


class Unit:
    def __init__(self, src, out, first=0, width=768, start=0, panels=4, tall=False, small=False):
        self.src, self.out, self.first, self.width, self.start, self.panels = src, out, first, width, start, panels
        self.tall, self.small = tall, small

    def block(self, b, half=None, n=1):
        if self.small:
            return self.src.at[pl.ds(b, n)] if n > 1 else self.src.at[b]
        w = self.width if half is None else self.width // 2
        C = pl.ds(self.first + (half or 0) * w, w)
        if self.tall:
            return self.src.at[b // 8, pl.ds(pl.multiple_of((b % 8) * 96, 8), 96 * n), C]
        return self.src.at[self.start : self.start + self.panels, pl.ds(pl.multiple_of(b * 24, 8), 24 * n), C]

    def chunk(self, b, k):
        if self.small:
            return self.src.at[b]
        if self.tall:
            return self.src.at[b // 8, pl.ds(pl.multiple_of((b % 8) * 96 + k * 24, 8), 24), :]
        return self.src.at[self.start + k, pl.ds(pl.multiple_of(b * 24, 8), 24), pl.ds(self.first, self.width)]

    def from_core(self, buf, zx, yy, k):
        if self.small:
            return buf.at[zx, yy]
        if self.tall:
            return buf.at[zx, pl.ds(pl.multiple_of(yy * 96 + k * 24, 8), 24), :]
        return buf.at[zx, k, pl.ds(pl.multiple_of(yy * 24, 8), 24), :]

    def arrived(self, buf, slot, k):
        if self.small:
            return buf.at[slot]
        if self.tall:
            return buf.at[slot, pl.ds(pl.multiple_of(k * 24, 8), 24), :]
        return buf.at[slot, k]

    def each(self, body):
        if self.small or self.panels == 1:
            body(0)
        else:
            pl.loop(0, self.panels)(body)


def unit_scratch(width=768, panels=4, tall=False, small=False):
    if small:
        one, half, two, t = (16, 128), (16, 128), (2, 16, 128), f32
    elif tall:
        one, half, two, t = (96, width), (96, width // 2), (192, width), bf
    else:
        one, half, two, t = (panels, 24, width), (panels, 24, width // 2), (panels, 48, width), bf
    return [pltpu.VMEM((n,) + d, t) for n, d in ((8, two), (4, half), (4, half), (4, one), (4, one), (5, one))]


UNITS = (dict(), dict(tall=True), dict(width=512, panels=3), dict(panels=1), dict(width=256, panels=3), dict(small=True))
PIECES = {1: (0,), 2: (1,), 3: (2, 3), 4: (4, 5)}


class Scatter(Pending):
    def __init__(self, units, bufs, ssem, rsem):
        self.sends = []
        self.units, self.ssem, self.rsem = units, ssem, rsem
        self.buf = [bufs[6 * p : 6 * p + 6] for p in range(len(units))]
        self.z, self.x, self.c, self.y = coords()
        self.to = neighbours()

    def rcopy(self, src, dst, p, j, k, to):
        zz = near(self.z, j)
        return remote(src, dst, self.ssem.at[p, j, k], self.rsem.at[p, zz, k], self.to[to])

    def send(self, p, j, k, where, to, half=None, n=1, when=None):
        def make():
            zz = near(self.z, j)
            if n == 2:
                xx, cc, yy = where, 1 - self.c, 0
            else:
                xx, cc, yy = (1 - self.x if where[0] else self.x), self.c, (1 - self.y if where[1] else self.y)
            src = self.units[p].block(block_of(zz, xx, cc, yy), half, n)
            if k < 2:
                dst = self.buf[p][0].at[zz * 2 + xx]
            elif k == RD:
                dst = self.buf[p][5].at[jnp.where(zz == self.z - 1, 4, zz)]
            else:
                dst = self.buf[p][k - 1].at[zz]
            return self.rcopy(src, dst, p, j, k, to)

        self.start(make, when)

    def wait(self, p, j, k, i, slot=None):
        zz = near(self.z, j)
        r = self.buf[p][i].at[zz if slot is None else slot]
        self.rcopy(r, r, p, j, k, "c").wait_recv()

    def wait_core(self, p, j, xx):
        zz = near(self.z, j)
        r = self.buf[p][0].at[zz * 2 + xx]
        self.rcopy(r, r, p, j, RC + xx, "c").wait_recv()

    def C(self, p, j):
        for xx in range(2):
            self.send(p, j, RC + xx, xx, "c", n=2)

    def D(self, p, j):
        z, x, c, y = self.z, self.x, self.c, self.y
        zz, u = near(z, j), self.units[p]
        self.wait_core(p, j, 1 - x)
        b = block_of(zz, 1 - x, c, 1 - y)

        def body(k):
            v = u.chunk(b, k)
            v[...] = (v[...].astype(f32) + u.from_core(self.buf[p][0], zz * 2 + 1 - x, 1 - y, k)[...].astype(f32)).astype(v.dtype)

        u.each(body)
        self.send(p, j, RDA, (1, 1), "y", half=None if u.small else 0)
        if not u.small:
            self.send(p, j, RDB, (1, 1), "x", half=1)

    def half_add(self, p, b, zx, yy, zz, half):
        r, u = self.buf[p][1 + half], self.units[p]

        def put(k, cut, extra):
            v = u.chunk(b, k).at[:, cut]
            w = u.from_core(self.buf[p][0], zx, yy, k).at[:, cut]
            s = v[...].astype(f32) + w[...].astype(f32)
            if extra is not None:
                s = s + extra[...].astype(f32)
            v[...] = s.astype(v.dtype)

        def body(k):
            if u.small:
                put(0, slice(0, 128), r.at[zz] if half == 0 else None)
            else:
                w = u.width // 2
                put(k, slice(half * w, half * w + w), u.arrived(r, zz, k))
                put(k, slice((1 - half) * w, (1 - half) * w + w), None)

        u.each(body)

    def X(self, p, j):
        z, x, c, y = self.z, self.x, self.c, self.y
        zz, u = near(z, j), self.units[p]
        self.wait(p, j, RDA, 1)
        self.half_add(p, block_of(zz, 1 - x, c, y), zz * 2 + 1 - x, y, zz, 0)
        self.send(p, j, RX, (1, 0), "x")
        self.wait_core(p, j, x)
        if not u.small:
            self.wait(p, j, RDB, 2)
        self.half_add(p, block_of(zz, x, c, 1 - y), zz * 2 + x, 1 - y, zz, 1)
        self.send(p, j, RY, (0, 1), "y")

    def O(self, p, j):
        z, x, c, y = self.z, self.x, self.c, self.y
        zz, u, B = near(z, j), self.units[p], self.buf[p]
        b = block_of(zz, x, c, y)
        self.wait(p, j, RX, 3)
        self.wait(p, j, RY, 4)

        def run(extra, final=False):
            def body(k):
                t = u.chunk(b, k)[...].astype(f32) + u.from_core(B[0], zz * 2 + x, y, k)[...].astype(f32)
                for e, slot in [(B[3], zz), (B[4], zz)] + [(B[5], i) for i in extra]:
                    t = t + u.arrived(e, slot, k)[...].astype(f32)
                v = u.out(k) if final else u.chunk(b, k)
                v[...] = t.astype(v.dtype)

            u.each(body)

        if j == 0:

            @pl.when(z > 0)
            def _():
                self.wait(p, j, RU, 5)

            @pl.when(z < 3)
            def _():
                self.wait(p, j, RD, 5, 4)

            pl.when(z == 0)(lambda: run([4], True))
            pl.when(z == 3)(lambda: run([zz], True))
            pl.when(jnp.logical_and(z > 0, z < 3))(lambda: run([zz, 4], True))
        else:
            up, down = zz > z, zz < z

            @pl.when(jnp.logical_and(up, z > 0))
            def _():
                self.wait(p, j, RU, 5)
                run([zz])

            @pl.when(jnp.logical_and(down, z < 3))
            def _():
                self.wait(p, j, RD, 5)
                run([zz])

            pl.when(jnp.logical_or(jnp.logical_and(up, z == 0), jnp.logical_and(down, z == 3)))(lambda: run([]))
            self.send(p, j, RU, (0, 0), "u", when=lambda: near(z, j) > z)
            self.send(p, j, RD, (0, 0), "d", when=lambda: near(z, j) < z)


PLAN = dict(
    start="S00S10S01S02T01S03T00T02T03U00U01S12W01W00S11S20",
    xt=((5, "U03U02W03W02"),),
    qkv=((4, "T10S13"), (7, "T12"),),
    attend=((0, "T11"), (1, "S21"), (2, "T20T13S22"), (5, "U10"),),
    out=((0, "T21"), (2, "U11U12U13"),),
    norm1=((7, "S23W13W11"),),
    ft=((5, "W12W10T22"),),
    up=((1, "U20"), (5, "U21"), (6, "T23"), (8, "U22"), (9, "W20"),),
    down=((0, "W22W21U23"), (2, "W23"),),
    norm2=(),
    gdn=((6, "C23"),),
    dact=((0, "C21"), (3, "D23"), (6, "C22"), (9, "D21"),),
    uback=((2, "D22X23"),),
    ugrad=((3, "X21C20"), (11, "C13C12"),),
    n1b=((7, "C11D20X22"),),
    oback=((1, "C10D13"),),
    aback=((1, "D12X20"),),
    qgrad=((0, "D11"), (3, "X13"), (5, "C33"),),
    bback=((0, "X12O23D33D10"), (1, "C32X11"),),
    rgrad=((1, "O22C31D32"), (2, "C30C41C43D31X33O21"),),
    igrad=((0, "D43"), (1, "D41O12C42C40D30D42X32O13D40"), (2, "X43O33X31X41O11X42X10X30O43X40O32O31O20O41O42O10O30O40"),),
)


class Steps:
    def __init__(self):
        self.gather = self.scatter = None

    def run(self, codes):
        for i in range(0, len(codes), 3):
            what, p, j = codes[i], int(codes[i + 1]), int(codes[i + 2])
            if what in "STUW":
                f = dict(S=self.gather.S, T=self.gather.T, U=self.gather.U, W=self.gather.W)[what]
                f(p, j)
            else:
                f = dict(C=self.scatter.C, D=self.scatter.D, X=self.scatter.X, O=self.scatter.O)[what]
                for u in PIECES[p]:
                    f(u, j)

    def loop(self, n, body, name):
        after = PLAN[name]

        def run(i):
            body(i)
            for k, codes in after:
                if k < n - 1:
                    pl.when(i == k)(lambda codes=codes: self.run(codes))

        pl.loop(0, n)(run)
        for k, codes in after:
            if k == n - 1:
                self.run(codes)


def lanes_in(tile, o, width, acc, t):
    lane = lax.broadcasted_iota(jnp.int32, tile.shape, 1)
    r = pltpu.roll(tile, o, axis=1) if o else tile
    acc[t] = jnp.where(jnp.logical_and(lane >= o, lane < o + width), r, acc[t])
    if o + width > 128:
        acc[t + 1] = jnp.where(lane < o + width - 128, r, acc[t + 1])


def lanes_out(acc, t, o, width):
    if not o:
        return acc[t]
    lane = lax.broadcasted_iota(jnp.int32, acc[t].shape, 1)
    r = pltpu.roll(acc[t], 128 - o, axis=1)
    if o + width > 128:
        r = jnp.where(lane < 128 - o, r, pltpu.roll(acc[t + 1], 128 - o, axis=1))
    return r


def small_to_rows(small, brow, upb):
    acc = [jnp.zeros((8, 128), f32)] * 6
    ups = [jnp.zeros((8, 128), f32)] * 24
    for b in range(32):
        lanes_in(small[b, 0:8, :], (24 * b) % 128, 24, acc, 24 * b // 128)
        lanes_in(small[b, 8:16, :], (96 * b) % 128, 96, ups, 96 * b // 128)
    for t in range(6):
        brow[:, t * 128 : t * 128 + 128] = acc[t]
    for t in range(24):
        upb[t // 6, 0:1, (t % 6) * 128 : (t % 6) * 128 + 128] = ups[t][0:1]


def rows_to_small(sums, gub, small):
    acc = [sums[:, t * 128 : t * 128 + 128] for t in range(6)]
    ups = [jnp.broadcast_to(gub[t // 6, 0:1, (t % 6) * 128 : (t % 6) * 128 + 128], (8, 128)) for t in range(24)]
    for b in range(32):
        small[b, 0:8, :] = lanes_out(acc, 24 * b // 128, (24 * b) % 128, 24)
        small[b, 8:16, :] = lanes_out(ups, 96 * b // 128, (96 * b) % 128, 96)


def layer_kernel(names, *refs):
    r = dict(zip(names, refs, strict=True))
    z, x, c, y = coords()
    b = block_of(z, x, c, y)
    moves = [(r["qkv_in"], r["w4"].at[0:3, rows(b, 24), :]), (r["out_in"], r["w4"].at[3, rows(b, 24), :])]
    moves += [(r["up_in"].at[:, n * 768 : n * 768 + 768], r["up"].at[n, rows(b, 24), :]) for n in range(4)]
    moves += [(r["dn_in"], block_ref(r["dn"], 2, b)), (r["x_in"], r["x"]), (r["dy_in"], r["dy"])]
    own = [pltpu.make_async_copy(s, d, r["lsem"].at[i]) for i, (s, d) in enumerate(moves)]
    for d in own:
        d.start()
    r["tile"][0:6, 0:24] = r["bias_in"][...].astype(f32)
    r["tile"][6:8, 0:24] = r["gain_in"][...].astype(f32)
    r["tile"][8:9, 0:96] = r["ub_in"][...].astype(f32)
    r["small"][b] = r["tile"][...]
    entry_barrier(z, x, c, y)
    for d in own:
        d.wait()

    out = [pltpu.make_async_copy(r[s], r[d], r["osem"].at[i]) for i, (s, d) in enumerate(zip(RESULTS, OUTPUTS))]
    steps = Steps()
    layer = Layer(r, steps.loop)
    g = steps.gather = Gather((r["w4"], r["up"], r["dn"], r["small"]), r["g_ssem"], r["g_rsem"], r["g_csem"])
    sources = [r[n] for n in ("dn", "g", "up", "up", "up", "small_g")]
    results = [
        lambda k: r["s_up"].at[:, pl.ds(pl.multiple_of(k * 768, 128), 768)],
        lambda k: r["s_dn"].at[rows(k, 24), :],
        lambda k: r["s_qkv"].at[k, :, 0:512],
        lambda k: r["s_out"],
        lambda k: r["s_qkv"].at[k, :, 512:768],
        lambda k: r["s_small"],
    ]
    places = (dict(), dict(), dict(), dict(start=3), dict(first=512), dict())
    units = [Unit(s, o, **form, **at) for s, o, form, at in zip(sources, results, UNITS, places)]
    s = steps.scatter = Scatter(units, [r[f"buf{i}"] for i in range(6 * len(UNITS))], r["s_ssem"], r["s_rsem"])

    layer.prepare()
    steps.run(PLAN["start"])
    layer.transpose(r["x"], r["xt"], "xt")
    small_to_rows(r["small"], r["brow"], r["upb"])
    layer.qkv()
    layer.attend()
    layer.out_proj()
    layer.norm_one()
    layer.transpose(r["a0"], r["ft"], "ft")
    layer.up_proj()
    layer.down_proj(lambda m: pick(z, m))
    layer.norm_two()
    out[0].start()
    layer.down_grad(lambda m: pick(z, 3 - m))
    layer.down_back()
    g.drain()
    layer.up_back()
    layer.up_grad()
    layer.norm_one_back()
    layer.out_back()
    layer.attend_back(0, 4, "aback")
    layer.qkv_grad(0, 2, "qgrad")
    layer.attend_back(4, 2, "bback")
    rows_to_small(r["sums"], r["gub"], r["small_g"])
    layer.qkv_grad(2, 1, "rgrad")
    layer.input_grad()
    for d in out[1:]:
        d.start()
    s.drain()
    for d in out:
        d.wait()


def pick(z, m):
    return sum(jnp.where(m == i, near(z, i), 0) for i in range(4))


RESULTS = ("o_act", "h", "s_qkv", "s_out", "s_up", "s_dn", "s_small")
OUTPUTS = ("y_act", "y_in", "y_qkv", "y_out", "y_up", "y_dn", "y_small")


def hand_on(*refs):
    a, small, o, bias, gain, ub = refs[:6], refs[6], refs[7:13], refs[13], refs[14], refs[15]
    via, sem = refs[16:22], refs[22]
    loads = [pltpu.make_async_copy(s, v, sem.at[0, i]) for i, (s, v) in enumerate(zip(a, via))]
    stores = [pltpu.make_async_copy(v, d, sem.at[1, i]) for i, (v, d) in enumerate(zip(via, o))]
    for d in loads:
        d.start()
    bias[...] = small[0:6, 0:24]
    gain[...] = small[6:8, 0:24]
    ub[...] = small[8:9, 0:96]
    for d, e in zip(loads, stores):
        d.wait()
        e.start()
    for e in stores:
        e.wait()


def body_chips(inputs, segment_ids, qkv_weight, out_weight, up_weight, down_weight, biases, gains, up_bias, out_grad):
    V, S, D = pltpu.VMEM, jax.ShapeDtypeStruct, pltpu.SemaphoreType.DMA
    vmem, hbm = pl.BlockSpec(memory_space=V), pl.BlockSpec(memory_space=pl.ANY)
    ins = dict(
        x_in=(inputs[0], hbm), seg=(segment_ids, vmem), dy_in=(out_grad[0], hbm), qkv_in=(qkv_weight, hbm), out_in=(out_weight, hbm), up_in=(up_weight, hbm),
        dn_in=(down_weight, hbm), bias_in=(biases, vmem), gain_in=(gains, vmem), ub_in=(up_bias.reshape(1, 96), vmem),
    )
    forms = (
        S((512, 768), bf), S((512, 768), f32), S((3, 24, 768), f32), S((24, 768), f32), S((24, 3072), f32), S((96, 768), f32), S((16, 128), f32),
    )
    big = V((4, 768, 768), bf)
    scratch = dict(
        layer_scratch(), x=V((512, 768), bf), dy=V((512, 768), bf), w4=big, up=big, dn=big, g=big, small=V((32, 16, 128), f32),
        small_g=V((32, 16, 128), f32), tile=V((16, 128), f32), brow=V((8, 768), f32), upb=V((4, 1, 768), f32), sums=V((8, 768), f32),
        gub=V((4, 1, 768), f32), lsem=D((9,)), osem=D((7,)), g_ssem=D((4, 4, 10)), g_rsem=D((4, 4, 5)), g_csem=D((4, 4, 4)),
        s_ssem=D((6, 4, 8)), s_rsem=D((6, 4, 8)), **{n: V(f.shape, f.dtype) for n, f in zip(RESULTS, forms)},
    )
    bufs = [b for form in UNITS for b in unit_scratch(**form)]
    scratch.update({f"buf{i}": b for i, b in enumerate(bufs)})
    names = list(ins) + list(OUTPUTS) + list(scratch)
    o = pl.pallas_call(
        functools.partial(layer_kernel, names),
        out_shape=forms,
        in_specs=[spec for _, spec in ins.values()],
        out_specs=[hbm] * len(forms),
        scratch_shapes=list(scratch.values()),
        compiler_params=pltpu.CompilerParams(collective_id=0, has_side_effects=True, vmem_limit_bytes=60 << 20),
        name="layer",
    )(*[a for a, _ in ins.values()])
    act, grad, qkv, out, up, dn, bias, gain, ub = pl.pallas_call(
        hand_on,
        out_shape=forms[:6] + (S((6, 24), f32), S((2, 24), f32), S((1, 96), f32)),
        in_specs=[hbm] * 6 + [vmem],
        out_specs=[hbm] * 6 + [vmem] * 3,
        scratch_shapes=[V(f.shape, f.dtype) for f in forms[:6]] + [D((2, 6))],
        name="hand_on",
    )(*o)
    return (act[None], grad[None], qkv, out, up, dn, bias, gain, ub.reshape(96))


def solution(mesh):
    chips = mesh.shape["wide"] == 16 and mesh.shape["narrow"] == 2
    return jax.shard_map(
        body_chips if chips else body_any,
        mesh=mesh,
        in_specs=(
            P(("wide", "narrow"), None, None),
            P(("wide", "narrow"), None),
            P(None, ("wide", "narrow"), None),
            P(("wide", "narrow"), None),
            P(("wide", "narrow"), None),
            P(("wide", "narrow"), None),
            P(None, ("wide", "narrow")),
            P(None, ("wide", "narrow")),
            P(("wide", "narrow")),
            P(("wide", "narrow"), None, None),
        ),
        out_specs=(
            P(("wide", "narrow"), None, None),
            P(("wide", "narrow"), None, None),
            P(None, ("wide", "narrow"), None),
            P(("wide", "narrow"), None),
            P(("wide", "narrow"), None),
            P(("wide", "narrow"), None),
            P(None, ("wide", "narrow")),
            P(None, ("wide", "narrow")),
            P(("wide", "narrow")),
        ),
        check_vma=False,
    )
```
